32 devices in a mesh: dom: 8 (over y, x, core), col: 4 (over z).
Axes of the slice: x: 2, y: 2, z: 4, core: 2. Of those that a mesh axis runs over, the one named last changes fastest.
Arguments:
- basis_panel: bfloat16 [256, 163840], P('col', 'dom'), may hold values from -12 to 12
- jacobian: bfloat16 [2, 320, 16384], P(None, None, 'dom'), may hold values from -0.25 to 0.25
- neighbors: int32 [512, 2], P('dom'), may hold values from 0 to 63
- sample_rows: int32 [16384], P('dom'), may hold values from 0 to 8191, as said below
- residual_parts: float32 [16384], P('dom'), may hold values from -48 to 48
Outputs:
- jacobian_basis: float32 [256, 8192], P('col', 'dom')
- sampled_residual: float32 [8192], P('dom')
- reduced_step: float32 [256], P('col')
The draws below stay inside these ranges and needn't reach their ends.
Inputs may be any that keep to these rules, and one draw needn't show every extreme that they name: `sample_rows`: for each index d of dom, its 2048 entries name each of its own rows d * 1024 to d * 1024 + 1023 exactly once; the other 1024 entries name rows owned by the 7 indices d + 1 to d + 7 of dom, cyclically, at most 256 to any one of them and exactly 256 to one of them. `neighbors`: each entry is an element of the same index of dom, counted from that index's first element.
All inputs are finite; a program needn't handle non-finite values.
Results may differ from the reference program's by a relative error of at most 0.0003.
Values sent between devices are 32-bit elements; how exact they have to be, the bound alone decides.
A program may use at most 64 MiB of HBM per device.

```python
import jax
import jax.numpy as jnp
from jax import lax

K = 256
NODE = 320
NB = 2
RS = 32
E_DEV = 64
ROWS_DEV = 1024
CAP = 256
REACH = 7
N_ELEM = 512
SAMPLES = 8192
DOFS = 163840
N_DOM = 8


def rows_of_device(key, device):
    keys = jax.random.split(jax.random.fold_in(key, device), 5)
    busy_offset = jax.random.randint(keys[0], (), 1, REACH + 1)
    spread = jnp.arange(REACH - 1, dtype=jnp.int32)
    others = 1 + (busy_offset + spread) % REACH
    chosen = jax.random.permutation(keys[1], (REACH - 1) * CAP)[:ROWS_DEV - CAP]
    offsets = jnp.concatenate([jnp.zeros((ROWS_DEV,), jnp.int32), jnp.full((CAP,), busy_offset, jnp.int32), others[chosen // CAP]])
    local_rows = jnp.concatenate([jax.random.permutation(keys[2], ROWS_DEV), jax.random.randint(keys[3], (ROWS_DEV,), 0, ROWS_DEV)])
    owners = (device + offsets) % N_DOM
    mixing = jax.random.permutation(keys[4], 2 * ROWS_DEV)
    return (owners * ROWS_DEV + local_rows)[mixing].astype(jnp.int32)


def draw_sample_rows(key, part):
    devices = jnp.arange(N_DOM, dtype=jnp.int32)
    return jax.vmap(lambda device: rows_of_device(key, device))(devices).reshape(-1)


def draw_basis_panel(key, part):
    keys = jax.random.split(key, 3)
    noise = jax.random.truncated_normal(keys[0], -5.0, 5.0, (K, DOFS), jnp.float32)
    weights = jax.random.uniform(keys[1], (K, 1), jnp.float32, 0.5, 1.5)
    shared = jax.random.truncated_normal(keys[2], -5.0, 5.0, (1, DOFS), jnp.float32)
    return (noise + 0.6 * weights * shared).astype(jnp.bfloat16)


def set_ends(result, rng, least, high):
    longest = result.shape.index(max(result.shape))
    spots = []
    for shift in (0, 1):
        where = [jax.random.randint(jax.random.fold_in(rng, axis), (), 0, length) for axis, length in enumerate(result.shape)]
        where[longest] = (where[longest] + shift) % result.shape[longest]
        spots.append(tuple(where))
    return result.at[spots[0]].set(least).at[spots[1]].set(high)


def shard_levels(rng, extent, shards, low, high):
    loudness, own = 1.0, jax.random.fold_in(rng, 6)
    for position, blocks in shards:
        steps = jnp.exp(jax.random.uniform(jax.random.fold_in(own, position), (blocks,), jnp.float32, low / len(shards), high / len(shards)))
        loudness = loudness * jnp.repeat(steps, extent[position] // blocks).reshape([-1 if axis == position else 1 for axis in range(len(extent))])
    return loudness


def scatter_about(rng, extent, width, limit, cuts=(), kind=jnp.bfloat16):
    drawn = jax.random.normal(rng, extent, jnp.float32) * width
    if len(cuts) > 0:
        drawn = shard_levels(rng, extent, cuts, -0.22, 0.18) * drawn
    return jnp.clip(drawn, min=-limit, max=limit).astype(kind)


def setup_inputs(seed: int = 0) -> dict:
    streams_of = jax.random.split(jax.random.key(seed), 6)
    return {
        "basis_panel": draw_basis_panel(jax.random.fold_in(streams_of[5], 71), 0),
        "jacobian": scatter_about(streams_of[1], (NB, NODE, N_ELEM * RS), (NB * NODE) ** -0.5, 0.25, ((2, 8),)),
        "neighbors": set_ends(jax.random.randint(streams_of[2], (N_ELEM, NB), 0, E_DEV), jax.random.fold_in(streams_of[2], 1), 0, E_DEV - 1).astype(jnp.int32),
        "sample_rows": draw_sample_rows(jax.random.fold_in(streams_of[5], 71), 0),
        "residual_parts": scatter_about(streams_of[4], (N_ELEM * RS,), 8.0, 48.0, ((0, 8),), jnp.float32),
    }


def reference(basis_panel, jacobian, neighbors, sample_rows, residual_parts):
    panels = basis_panel.reshape(K, N_DOM, E_DEV, NODE).transpose(1, 0, 2, 3)
    blocks = jacobian.reshape(NB, NODE, N_DOM, E_DEV, RS).transpose(2, 0, 1, 3, 4)
    links = neighbors.reshape(N_DOM, E_DEV, NB)

    def per_device(operands):
        panel_slab, block_slab, link_slab = operands
        summed = jnp.zeros((K, E_DEV, RS), jnp.float32)
        for coupled in range(NB):
            picked = jnp.take(panel_slab, link_slab[:, coupled], axis=1).astype(jnp.float32)
            summed = summed + jnp.einsum('cep,per->cer', picked, block_slab[coupled].astype(jnp.float32), precision=lax.Precision.HIGHEST)
        return summed.reshape(K, E_DEV * RS)
    partial_value = lax.map(per_device, (panels, blocks, links))
    partial_value = partial_value.transpose(1, 0, 2).reshape(K, N_ELEM * RS)
    jacobian_basis = jnp.zeros((K, SAMPLES), jnp.float32).at[:, sample_rows].add(partial_value)
    sampled_residual = jnp.zeros((SAMPLES,), jnp.float32).at[sample_rows].add(residual_parts)
    gram_matrix = jnp.einsum('kr,lr->kl', jacobian_basis, jacobian_basis, precision=lax.Precision.HIGHEST)
    gradient = jnp.einsum('kr,r->k', jacobian_basis, sampled_residual, precision=lax.Precision.HIGHEST)
    factor = jnp.linalg.cholesky(gram_matrix)
    forward = lax.linalg.triangular_solve(factor, gradient[:, None], left_side=True, lower=True)
    backward = lax.linalg.triangular_solve(factor, forward, left_side=True, lower=True, transpose_a=True)
    reduced_step = -backward[:, 0]
    return (jacobian_basis, sampled_residual, reduced_step)
```

```python
import functools

import jax
import jax.numpy as jnp
from jax import lax
from jax.experimental import pallas as pl
from jax.experimental.pallas import tpu as pltpu
from jax.sharding import PartitionSpec as P

ROWS_DEV = 1024
CAP = 256
LANES = 128
HIGHEST = lax.Precision.HIGHEST
F32 = jnp.float32
BF16 = jnp.bfloat16


def iota(shape, dim):
    return lax.broadcasted_iota(jnp.int32, shape, dim)


def dot_nn(a, b, precision=None):
    return lax.dot_general(
        a, b, (((1,), (0,)), ((), ())), precision=precision, preferred_element_type=F32
    )


def dot_nt(a, b, precision=None):
    return lax.dot_general(
        a, b, (((1,), (1,)), ((), ())), precision=precision, preferred_element_type=F32
    )


def dot_tn(a, b, precision=None):
    return lax.dot_general(
        a, b, (((0,), (0,)), ((), ())), precision=precision, preferred_element_type=F32
    )


def split_values(x):
    high = x.astype(BF16)
    return high, (x - high.astype(F32)).astype(BF16)


def split_extra(x):
    high = x.astype(BF16).astype(F32)
    middle = (x - high).astype(BF16).astype(F32)
    low = x - high - middle
    return jnp.concatenate([high, middle, low, jnp.zeros_like(x)], axis=0).astype(BF16)


def join(found, width):
    values = found[:width] + found[width : 2 * width]
    base = 2 * width
    extra = found[base : base + 8] + found[base + 8 : base + 16] + found[base + 16 : base + 24]
    return jnp.concatenate([values, extra], axis=0)


def pick(terms, targets, base):
    spots = iota((CAP, targets.shape[1]), 0) + base
    return dot_nt(terms, (spots == targets).astype(F32).astype(BF16))


def product_kernel(
    dom_count, self_ref, links_ref, panel_ref, blocks_ref, rows_ref, parts_ref,
    local_ref, send_ref, panels, terms,
):
    width = panel_ref.shape[0]
    coupled_count, node, entries = blocks_ref.shape
    elements = links_ref.shape[0]
    rs = entries // elements
    group = LANES // rs

    @pl.loop(0, elements // 2)
    def _(pair):
        window = panel_ref[:, pl.ds(pl.multiple_of(pair * 2 * node, LANES), 2 * node)]
        panels[2 * pair] = window[:, :node]
        panels[2 * pair + 1] = window[:, node:]

    lane_element = iota((width, LANES), 1) // rs

    @pl.loop(0, elements // group)
    def _(block):
        columns = pl.ds(pl.multiple_of(block * LANES, LANES), LANES)
        total = jnp.zeros((group * width, LANES), F32)
        for coupled in range(coupled_count):
            picked = jnp.concatenate(
                [panels[links_ref[block * group + q, coupled]] for q in range(group)], axis=0
            )
            total = total + dot_nn(picked, blocks_ref[coupled, :, columns])
        out = total[:width]
        for q in range(1, group):
            out = jnp.where(lane_element == q, total[q * width : (q + 1) * width], out)
        high, low = split_values(out)
        terms[:width, columns] = high
        terms[width : 2 * width, columns] = low

    own = self_ref[0]
    shift = ROWS_DEV.bit_length() - 1
    match_rows = max(16, dom_count)
    before = (iota((LANES, LANES), 0) < iota((LANES, LANES), 1)).astype(F32).astype(BF16)
    carry = jnp.zeros((match_rows, 1), F32)
    targets = []
    for start in range(0, entries, LANES):
        rows = rows_ref[:, start : start + LANES]
        owner = rows >> shift
        local_row = rows & (ROWS_DEV - 1)
        matches = (iota((match_rows, LANES), 0) == owner).astype(F32)
        ranks = jnp.sum(
            matches * (dot_nn(matches.astype(BF16), before) + carry), axis=0, keepdims=True
        ).astype(jnp.int32)
        carry = carry + jnp.sum(matches, axis=1, keepdims=True)
        targets.append(jnp.where(owner == own, local_row, ROWS_DEV + owner * CAP + ranks))
    targets = jnp.concatenate(targets, axis=1)

    row_values = (rows_ref[...] & (ROWS_DEV - 1)).astype(F32)
    which = iota((8, entries), 0)
    extra = jnp.where(which == 0, parts_ref[...], jnp.where(which == 1, row_values, 0.0))
    terms[2 * width :, :] = split_extra(extra)

    @pl.loop(0, ROWS_DEV // CAP)
    def _(tile):
        base = tile * CAP
        local_ref[:, pl.ds(pl.multiple_of(base, CAP), CAP)] = join(
            pick(terms[...], targets, base), width
        )

    @pl.loop(0, dom_count)
    def _(owner):
        send_ref[owner] = join(pick(terms[...], targets, ROWS_DEV + owner * CAP), width)


def assemble_kernel(local_ref, arrived_ref, basis_ref, residual_ref, split_ref, terms, landing):
    sources, height, _ = arrived_ref.shape
    width = height - 8
    for source in range(sources):
        columns = slice(source * CAP, (source + 1) * CAP)
        high, low = split_values(arrived_ref[source, :width, :])
        terms[:width, columns] = high
        terms[width : 2 * width, columns] = low
        extra = arrived_ref[source, width:, :]
        terms[2 * width :, columns] = split_extra(extra)
        landing[:, columns] = extra[1:2, :].astype(jnp.int32)
    targets = landing[...]
    for tile in range(ROWS_DEV // CAP):
        columns = slice(tile * CAP, (tile + 1) * CAP)
        total = join(pick(terms[...], targets, tile * CAP), width) + local_ref[:, columns]
        basis_ref[:, columns] = total[:width]
        residual_ref[:, columns] = total[width : width + 1]
    part = split_ref.shape[2]
    for index in range(split_ref.shape[0]):
        split_ref[index] = basis_ref[:, index * part : (index + 1) * part]


def gram_kernel(basis_ref, residual_ref, out_ref):
    basis = basis_ref[...]
    size = basis.shape[0]
    gram = dot_nt(basis, basis, HIGHEST)
    residual = jnp.broadcast_to(residual_ref[...], (8, basis.shape[1]))
    gradient = dot_nt(residual, basis, HIGHEST)[:1]
    row, column = iota((size, size), 0), iota((size, size), 1)
    gram = jnp.where((row == size - 1) & (column < size - 1), gradient, gram)
    turned = pltpu.roll(jnp.broadcast_to(gradient, (8, size)), 1, axis=1)[:1]
    out_ref[...] = jnp.where((row == size - 2) & (column == 0), turned, gram)


def total_kernel(parts_ref, out_ref):
    total = jnp.sum(parts_ref[...], axis=0)
    for index in range(out_ref.shape[0]):
        out_ref[index] = total


def inverse(matrix):
    size = matrix.shape[0]
    shape = (8, size)
    row, lane = iota(shape, 0), iota(shape, 1)

    def step(_, groups):
        panel = groups[0]
        columns = [jnp.broadcast_to(panel[:, j : j + 1], shape) for j in range(8)]
        work = jnp.where(lane < 8, (lane == row).astype(F32), panel)
        for i in range(8):
            here = row == i
            scale = 1.0 / jnp.broadcast_to(columns[i][i : i + 1], shape)
            factor = columns[i]
            moved = jnp.broadcast_to(work[i : i + 1], shape) * scale
            work = jnp.where(here, moved, work - factor * moved)
            for j in range(i + 1, 8):
                moved = jnp.broadcast_to(columns[j][i : i + 1], shape) * scale
                columns[j] = jnp.where(here, moved, columns[j] - factor * moved)
        spread = [jnp.broadcast_to(work[k : k + 1], shape) for k in range(8)]
        done = []
        for other in groups[1:]:
            out = jnp.where(lane < 8, 0.0, other)
            for k in range(8):
                out = out - jnp.broadcast_to(other[:, k : k + 1], shape) * spread[k]
            done.append(out)
        return tuple(pltpu.roll(x, size - 8, axis=1) for x in done + [work])

    groups = tuple(matrix[k : k + 8] for k in range(0, size, 8))
    return jnp.concatenate(lax.fori_loop(0, size // 8, step, groups), axis=0)


def solve_kernel(gram_ref, out_ref):
    size = gram_ref.shape[0]
    half = size // 2
    row, column = iota((half, half), 0), iota((half, half), 1)
    upper = row <= column

    def mirrored(block):
        block = jnp.where(upper, block, 0.0)
        return block + jnp.where(row == column, 0.0, block).T

    lane = iota((1, size), 1)
    last = jnp.sum(
        jnp.where(lane == 0, gram_ref[size - 2 : size - 1, :], 0.0), axis=1, keepdims=True
    )
    gradient = jnp.where(lane == size - 1, last, gram_ref[size - 1 : size, :])
    gradient = jnp.broadcast_to(gradient, (8, size))
    first = mirrored(gram_ref[:half, :half])
    cross = gram_ref[:half, half:]
    second = mirrored(gram_ref[half:, half:])
    first_inverse = inverse(first)
    carried = dot_nn(first_inverse, cross, HIGHEST)
    second_inverse = inverse(second - dot_tn(cross, carried, HIGHEST))

    def apply(top, bottom):
        low = dot_nt(bottom - dot_nn(top, carried, HIGHEST), second_inverse, HIGHEST)
        return dot_nt(top, first_inverse, HIGHEST) - dot_nt(low, carried, HIGHEST), low

    top, bottom = gradient[:, :half], gradient[:, half:]
    x_top, x_bottom = apply(top, bottom)
    off_top = top - dot_nn(x_top, first, HIGHEST) - dot_nt(x_bottom, cross, HIGHEST)
    off_bottom = bottom - dot_nn(x_top, cross, HIGHEST) - dot_nn(x_bottom, second, HIGHEST)
    more_top, more_bottom = apply(off_top, off_bottom)
    out_ref[:, :half] = -(x_top + more_top)[:1]
    out_ref[:, half:] = -(x_bottom + more_bottom)[:1]


VMEM = pl.BlockSpec(memory_space=pltpu.VMEM)
SMEM = pl.BlockSpec(memory_space=pltpu.SMEM)


def body(basis_panel, jacobian, neighbors, sample_rows, residual_parts):
    dom_count, col_count = lax.axis_size("dom"), lax.axis_size("col")
    col_index = lax.axis_index("col")
    width = basis_panel.shape[0]
    entries = sample_rows.shape[0]
    elements = neighbors.shape[0]
    node = jacobian.shape[1]
    size = width * col_count
    shape = jax.ShapeDtypeStruct
    local, send = pl.pallas_call(
        functools.partial(product_kernel, dom_count),
        out_shape=(shape((width + 8, ROWS_DEV), F32), shape((dom_count, width + 8, CAP), F32)),
        in_specs=[SMEM, SMEM, VMEM, VMEM, VMEM, VMEM],
        out_specs=(VMEM, VMEM),
        scratch_shapes=[
            pltpu.VMEM((elements, width, node), BF16),
            pltpu.VMEM((2 * width + 32, entries), BF16),
        ],
        name="products",
    )(
        lax.axis_index("dom").astype(jnp.int32).reshape(1),
        neighbors,
        basis_panel,
        jacobian,
        sample_rows.reshape(1, entries),
        residual_parts.reshape(1, entries),
    )
    arrived = lax.all_to_all(send, "dom", split_axis=0, concat_axis=0, tiled=True)
    part = ROWS_DEV // col_count
    jacobian_basis, sampled_residual, pieces = pl.pallas_call(
        assemble_kernel,
        out_shape=(
            shape((width, ROWS_DEV), F32),
            shape((1, ROWS_DEV), F32),
            shape((col_count, width, part), F32),
        ),
        in_specs=[VMEM, VMEM],
        out_specs=(VMEM, VMEM, VMEM),
        scratch_shapes=[
            pltpu.VMEM((2 * width + 32, dom_count * CAP), BF16),
            pltpu.VMEM((1, dom_count * CAP), jnp.int32),
        ],
        name="assemble",
    )(local, arrived)
    pieces = lax.all_to_all(pieces, "col", split_axis=0, concat_axis=0, tiled=True)
    own_residual = lax.dynamic_slice_in_dim(sampled_residual, col_index * part, part, axis=1)
    gram = pl.pallas_call(
        gram_kernel,
        out_shape=shape((size, size), F32),
        in_specs=[VMEM, VMEM],
        out_specs=VMEM,
        name="gram",
    )(pieces.reshape(size, part), own_residual)
    devices = dom_count * col_count
    chunk = (devices, size // devices, size) if size % devices == 0 else (devices, 1, size * size // devices)
    spread = lax.all_to_all(
        gram.reshape(chunk), ("dom", "col"), split_axis=0, concat_axis=0, tiled=True
    )
    summed = pl.pallas_call(
        total_kernel, out_shape=shape(chunk, F32), in_specs=[VMEM], out_specs=VMEM, name="total"
    )(spread)
    whole = lax.all_to_all(summed, ("dom", "col"), split_axis=0, concat_axis=0, tiled=True)
    full_step = pl.pallas_call(
        solve_kernel,
        out_shape=shape((1, size), F32),
        in_specs=[VMEM],
        out_specs=VMEM,
        name="solve",
    )(whole.reshape(size, size))
    reduced_step = lax.dynamic_slice_in_dim(full_step[0], col_index * width, width)
    return (jacobian_basis, sampled_residual[0], reduced_step)


def solution(mesh):
    placed = (P("col", "dom"), P(None, None, "dom"), P("dom", None), P("dom"), P("dom"))
    return jax.shard_map(
        body,
        mesh=mesh,
        in_specs=placed,
        out_specs=(P("col", "dom"), P("dom"), P("col")),
        check_vma=False,
    )
```

```python
import functools

import jax
import jax.numpy as jnp
from jax import lax
from jax.experimental import pallas as pl
from jax.experimental.pallas import tpu as pltpu
from jax.sharding import PartitionSpec as P

ROWS_DEV = 1024
CAP = 256
REACH_MOST = 8
LANES = 128
HIGHEST = lax.Precision.HIGHEST
F32 = jnp.float32
BF16 = jnp.bfloat16


def iota(shape, dim):
    return lax.broadcasted_iota(jnp.int32, shape, dim)


def dot_nn(a, b, precision=None):
    return lax.dot_general(
        a, b, (((1,), (0,)), ((), ())), precision=precision, preferred_element_type=F32
    )


def dot_nt(a, b, precision=None):
    return lax.dot_general(
        a, b, (((1,), (1,)), ((), ())), precision=precision, preferred_element_type=F32
    )


def dot_tn(a, b, precision=None):
    return lax.dot_general(
        a, b, (((0,), (0,)), ((), ())), precision=precision, preferred_element_type=F32
    )


def split_values(x):
    high = x.astype(BF16)
    return high, (x - high.astype(F32)).astype(BF16)


def split_extra(x):
    high = x.astype(BF16).astype(F32)
    middle = (x - high).astype(BF16).astype(F32)
    low = x - high - middle
    return jnp.concatenate([high, middle, low, jnp.zeros_like(x)], axis=0).astype(BF16)


def join(found, width):
    values = found[:width] + found[width : 2 * width]
    base = 2 * width
    extra = found[base : base + 8] + found[base + 8 : base + 16] + found[base + 16 : base + 24]
    return jnp.concatenate([values, extra], axis=0)


def pick(terms, targets, base):
    spots = iota((CAP, targets.shape[1]), 0) + base
    return dot_nt(terms, (spots == targets).astype(F32).astype(BF16))


def fold(value, count):
    return jnp.where(value >= count, value - count, value)


def step_kernel(
    dom_count, col_count, reach, links_ref, panel_ref, blocks_ref, rows_ref, parts_ref,
    basis_ref, residual_ref, gram_ref,
    panels, terms, send, arrived, local, terms_in, landing, pieces, others, parts, sums, total,
    whole, dom_sems, col_sems, sum_sems, all_sems,
):
    dom, col = lax.axis_index("dom"), lax.axis_index("col")
    devices = dom_count * col_count
    me = dom * col_count + col
    width = panel_ref.shape[0]
    coupled_count, node, entries = blocks_ref.shape
    elements = links_ref.shape[0]
    rs = entries // elements
    group = LANES // rs
    part = ROWS_DEV // col_count
    size = width * col_count

    def remote(source, target, sems, index, device):
        return pltpu.make_async_remote_copy(
            src_ref=source,
            dst_ref=target,
            send_sem=sems.at[0, index],
            recv_sem=sems.at[1, index],
            device_id=device,
            device_id_type=pl.DeviceIdType.MESH,
        )

    def device_at(offset):
        index = fold(me + offset, devices)
        return index, (index // col_count, index % col_count)

    def dom_copy(o):
        return remote(send.at[o - 1], arrived.at[o - 1], dom_sems, o - 1, (fold(dom + o, dom_count), col))

    def col_copy(o):
        there = fold(col + o, col_count)
        return remote(pieces.at[there], others.at[col], col_sems, o - 1, (dom, there))

    def sum_copy(o):
        index, device = device_at(o)
        return remote(parts.at[index], sums.at[o - 1], sum_sems, o - 1, device)

    def all_copy(o):
        _, device = device_at(o)
        return remote(total, whole.at[me], all_sems, o - 1, device)

    barrier = pltpu.get_barrier_semaphore()

    @pl.loop(1, devices)
    def _(o):
        _, device = device_at(o)
        pl.semaphore_signal(barrier, inc=1, device_id=device, device_id_type=pl.DeviceIdType.MESH)

    @pl.loop(0, elements // 2)
    def _(pair):
        window = panel_ref[:, pl.ds(pl.multiple_of(pair * 2 * node, LANES), 2 * node)]
        panels[2 * pair] = window[:, :node]
        panels[2 * pair + 1] = window[:, node:]

    lane_element = iota((width, LANES), 1) // rs

    @pl.loop(0, elements // group)
    def _(block):
        columns = pl.ds(pl.multiple_of(block * LANES, LANES), LANES)
        found = jnp.zeros((group * width, LANES), F32)
        for coupled in range(coupled_count):
            picked = jnp.concatenate(
                [panels[links_ref[block * group + q, coupled]] for q in range(group)], axis=0
            )
            found = found + dot_nn(picked, blocks_ref[coupled, :, columns])
        out = found[:width]
        for q in range(1, group):
            out = jnp.where(lane_element == q, found[q * width : (q + 1) * width], out)
        high, low = split_values(out)
        terms[:width, columns] = high
        terms[width : 2 * width, columns] = low

    shift = ROWS_DEV.bit_length() - 1
    match_rows = max(16, dom_count)
    before = (iota((LANES, LANES), 0) < iota((LANES, LANES), 1)).astype(F32).astype(BF16)
    carry = jnp.zeros((match_rows, 1), F32)
    targets = []
    for start in range(0, entries, LANES):
        rows = rows_ref[:, start : start + LANES]
        offset = fold((rows >> shift) - dom + dom_count, dom_count)
        local_row = rows & (ROWS_DEV - 1)
        matches = (iota((match_rows, LANES), 0) == offset).astype(F32)
        ranks = jnp.sum(
            matches * (dot_nn(matches.astype(BF16), before) + carry), axis=0, keepdims=True
        ).astype(jnp.int32)
        carry = carry + jnp.sum(matches, axis=1, keepdims=True)
        targets.append(
            jnp.where(offset == 0, local_row, ROWS_DEV + (offset - 1) * CAP + ranks)
        )
    targets = jnp.concatenate(targets, axis=1)

    row_values = (rows_ref[...] & (ROWS_DEV - 1)).astype(F32)
    which = iota((8, entries), 0)
    extra = jnp.where(which == 0, parts_ref[...], jnp.where(which == 1, row_values, 0.0))
    terms[2 * width :, :] = split_extra(extra)

    pl.semaphore_wait(barrier, devices - 1)

    @pl.loop(1, reach + 1)
    def _(o):
        send[o - 1] = join(pick(terms[...], targets, ROWS_DEV + (o - 1) * CAP), width)
        dom_copy(o).start()

    @pl.loop(0, ROWS_DEV // CAP)
    def _(tile):
        base = tile * CAP
        local[:, pl.ds(pl.multiple_of(base, CAP), CAP)] = join(
            pick(terms[...], targets, base), width
        )

    for o in range(1, reach + 1):
        dom_copy(o).wait_recv()
        columns = slice((o - 1) * CAP, o * CAP)
        high, low = split_values(arrived[o - 1, :width, :])
        terms_in[:width, columns] = high
        terms_in[width : 2 * width, columns] = low
        extra = arrived[o - 1, width:, :]
        terms_in[2 * width :, columns] = split_extra(extra)
        landing[:, columns] = extra[1:2, :].astype(jnp.int32)
    targets = landing[...]

    def assemble(base):
        columns = pl.ds(pl.multiple_of(base, CAP), CAP)
        found = join(pick(terms_in[...], targets, base), width) + local[:, columns]
        basis_ref[:, columns] = found[:width]
        residual_ref[:, columns] = found[width : width + 1]
        return found

    if part == CAP:

        @pl.loop(1, col_count)
        def _(o):
            there = fold(col + o, col_count)
            pieces[there] = assemble(there * part)[:width]
            col_copy(o).start()

        found = assemble(col * part)
        others[col] = found[:width]
        own_residual = found[width : width + 1]
    else:
        for tile in range(ROWS_DEV // CAP):
            assemble(tile * CAP)
        own_residual = jnp.zeros((1, part), F32)
        for index in range(col_count):
            columns = slice(index * part, (index + 1) * part)
            pieces[index] = basis_ref[:, columns]
            own_residual = own_residual + jnp.where(index == col, residual_ref[:, columns], 0.0)
        for o in range(1, col_count):
            col_copy(o).start()
        others[col] = pieces[col]
    for o in range(1, col_count):
        col_copy(o).wait_recv()

    basis = others[...].reshape(size, part)
    gram = dot_nt(basis, basis, HIGHEST)
    gradient = dot_nt(jnp.broadcast_to(own_residual, (8, part)), basis, HIGHEST)[:1]
    row, column = iota((size, size), 0), iota((size, size), 1)
    gram = jnp.where((row == size - 1) & (column < size - 1), gradient, gram)
    turned = pltpu.roll(jnp.broadcast_to(gradient, (8, size)), 1, axis=1)[:1]
    gram = jnp.where((row == size - 2) & (column == 0), turned, gram)
    count, height, span = parts.shape
    if span == size:
        for index in range(count):
            parts[index] = gram[index * height : (index + 1) * height]
    else:
        for index in range(count):
            start = index * span % size
            parts[index] = gram[index * span // size][None, start : start + span]

    @pl.loop(1, devices)
    def _(o):
        sum_copy(o).start()

    @pl.loop(1, devices)
    def _(o):
        sum_copy(o).wait_recv()

    mine = jnp.sum(sums[...], axis=0) + parts[me]
    total[...] = mine

    @pl.loop(1, devices)
    def _(o):
        all_copy(o).start()

    whole[me] = mine

    @pl.loop(1, devices)
    def _(o):
        all_copy(o).wait_recv()

    gram_ref[...] = whole[...]
    for o in range(1, reach + 1):
        dom_copy(o).wait_send()
    for o in range(1, col_count):
        col_copy(o).wait_send()

    @pl.loop(1, devices)
    def _(o):
        sum_copy(o).wait_send()
        all_copy(o).wait_send()


def inverse(matrix):
    size = matrix.shape[0]
    shape = (8, size)
    row, lane = iota(shape, 0), iota(shape, 1)

    def step(_, groups):
        panel = groups[0]
        columns = [jnp.broadcast_to(panel[:, j : j + 1], shape) for j in range(8)]
        work = jnp.where(lane < 8, (lane == row).astype(F32), panel)
        for i in range(8):
            here = row == i
            scale = 1.0 / jnp.broadcast_to(columns[i][i : i + 1], shape)
            factor = columns[i]
            moved = jnp.broadcast_to(work[i : i + 1], shape) * scale
            work = jnp.where(here, moved, work - factor * moved)
            for j in range(i + 1, 8):
                moved = jnp.broadcast_to(columns[j][i : i + 1], shape) * scale
                columns[j] = jnp.where(here, moved, columns[j] - factor * moved)
        spread = [jnp.broadcast_to(work[k : k + 1], shape) for k in range(8)]
        done = []
        for other in groups[1:]:
            out = jnp.where(lane < 8, 0.0, other)
            for k in range(8):
                out = out - jnp.broadcast_to(other[:, k : k + 1], shape) * spread[k]
            done.append(out)
        return tuple(pltpu.roll(x, size - 8, axis=1) for x in done + [work])

    groups = tuple(matrix[k : k + 8] for k in range(0, size, 8))
    return jnp.concatenate(lax.fori_loop(0, size // 8, step, groups), axis=0)


def solve_kernel(gram_ref, out_ref):
    size = gram_ref.shape[0]
    half = size // 2
    row, column = iota((half, half), 0), iota((half, half), 1)
    upper = row <= column

    def mirrored(block):
        block = jnp.where(upper, block, 0.0)
        return block + jnp.where(row == column, 0.0, block).T

    lane = iota((1, size), 1)
    last = jnp.sum(
        jnp.where(lane == 0, gram_ref[size - 2 : size - 1, :], 0.0), axis=1, keepdims=True
    )
    gradient = jnp.where(lane == size - 1, last, gram_ref[size - 1 : size, :])
    gradient = jnp.broadcast_to(gradient, (8, size))
    first = mirrored(gram_ref[:half, :half])
    cross = gram_ref[:half, half:]
    second = mirrored(gram_ref[half:, half:])
    first_inverse = inverse(first)
    carried = dot_nn(first_inverse, cross, HIGHEST)
    second_inverse = inverse(second - dot_tn(cross, carried, HIGHEST))

    def apply(top, bottom):
        low = dot_nt(bottom - dot_nn(top, carried, HIGHEST), second_inverse, HIGHEST)
        return dot_nt(top, first_inverse, HIGHEST) - dot_nt(low, carried, HIGHEST), low

    top, bottom = gradient[:, :half], gradient[:, half:]
    x_top, x_bottom = apply(top, bottom)
    off_top = top - dot_nn(x_top, first, HIGHEST) - dot_nt(x_bottom, cross, HIGHEST)
    off_bottom = bottom - dot_nn(x_top, cross, HIGHEST) - dot_nn(x_bottom, second, HIGHEST)
    more_top, more_bottom = apply(off_top, off_bottom)
    out_ref[:, :half] = -(x_top + more_top)[:1]
    out_ref[:, half:] = -(x_bottom + more_bottom)[:1]


VMEM = pl.BlockSpec(memory_space=pltpu.VMEM)
SMEM = pl.BlockSpec(memory_space=pltpu.SMEM)


def body(basis_panel, jacobian, neighbors, sample_rows, residual_parts):
    dom_count, col_count = lax.axis_size("dom"), lax.axis_size("col")
    col_index = lax.axis_index("col")
    width = basis_panel.shape[0]
    entries = sample_rows.shape[0]
    elements = neighbors.shape[0]
    node = jacobian.shape[1]
    size = width * col_count
    shape = jax.ShapeDtypeStruct
    reach = min(dom_count - 1, REACH_MOST)
    part = ROWS_DEV // col_count
    devices = dom_count * col_count
    if size % devices == 0:
        chunk = (devices, size // devices, size)
    else:
        chunk = (devices, 1, size * size // devices)
    jacobian_basis, sampled_residual, whole = pl.pallas_call(
        functools.partial(step_kernel, dom_count, col_count, reach),
        out_shape=(
            shape((width, ROWS_DEV), F32), shape((1, ROWS_DEV), F32), shape(chunk, F32)
        ),
        in_specs=[SMEM, VMEM, VMEM, VMEM, VMEM],
        out_specs=(VMEM, VMEM, VMEM),
        scratch_shapes=[
            pltpu.VMEM((elements, width, node), BF16),
            pltpu.VMEM((2 * width + 32, entries), BF16),
            pltpu.VMEM((reach, width + 8, CAP), F32),
            pltpu.VMEM((reach, width + 8, CAP), F32),
            pltpu.VMEM((width + 8, ROWS_DEV), F32),
            pltpu.VMEM((2 * width + 32, reach * CAP), BF16),
            pltpu.VMEM((1, reach * CAP), jnp.int32),
            pltpu.VMEM((col_count, width, part), F32),
            pltpu.VMEM((col_count, width, part), F32),
            pltpu.VMEM(chunk, F32),
            pltpu.VMEM((devices - 1,) + chunk[1:], F32),
            pltpu.VMEM(chunk[1:], F32),
            pltpu.VMEM(chunk, F32),
            pltpu.SemaphoreType.DMA((2, reach)),
            pltpu.SemaphoreType.DMA((2, col_count - 1)),
            pltpu.SemaphoreType.DMA((2, devices - 1)),
            pltpu.SemaphoreType.DMA((2, devices - 1)),
        ],
        compiler_params=pltpu.CompilerParams(collective_id=0, has_side_effects=True),
        name="step",
    )(
        neighbors,
        basis_panel,
        jacobian,
        sample_rows.reshape(1, entries),
        residual_parts.reshape(1, entries),
    )
    full_step = pl.pallas_call(
        solve_kernel,
        out_shape=shape((1, size), F32),
        in_specs=[VMEM],
        out_specs=VMEM,
        name="solve",
    )(whole.reshape(size, size))
    reduced_step = lax.dynamic_slice_in_dim(full_step[0], col_index * width, width)
    return (jacobian_basis, sampled_residual[0], reduced_step)


def solution(mesh):
    placed = (P("col", "dom"), P(None, None, "dom"), P("dom", None), P("dom"), P("dom"))
    return jax.shard_map(
        body,
        mesh=mesh,
        in_specs=placed,
        out_specs=(P("col", "dom"), P("dom"), P("col")),
        check_vma=False,
    )
```

```python
import functools

import jax
import jax.numpy as jnp
from jax import lax
from jax.experimental import pallas as pl
from jax.experimental.pallas import tpu as pltpu
from jax.sharding import PartitionSpec as P

ROWS_DEV = 1024
CAP = 256
REACH_MOST = 8
LANES = 128
HIGHEST = lax.Precision.HIGHEST
F32 = jnp.float32
BF16 = jnp.bfloat16


def iota(shape, dim):
    return lax.broadcasted_iota(jnp.int32, shape, dim)


def dot_nn(a, b, precision=None):
    return lax.dot_general(
        a, b, (((1,), (0,)), ((), ())), precision=precision, preferred_element_type=F32
    )


def dot_nt(a, b, precision=None):
    return lax.dot_general(
        a, b, (((1,), (1,)), ((), ())), precision=precision, preferred_element_type=F32
    )


def dot_tn(a, b, precision=None):
    return lax.dot_general(
        a, b, (((0,), (0,)), ((), ())), precision=precision, preferred_element_type=F32
    )


def split_values(x):
    high = x.astype(BF16)
    return high, (x - high.astype(F32)).astype(BF16)


def split_extra(x):
    high = x.astype(BF16).astype(F32)
    middle = (x - high).astype(BF16).astype(F32)
    low = x - high - middle
    return jnp.concatenate([high, middle, low, jnp.zeros_like(x)], axis=0).astype(BF16)


def join(found, width):
    values = found[:width] + found[width : 2 * width]
    base = 2 * width
    extra = found[base : base + 8] + found[base + 8 : base + 16] + found[base + 16 : base + 24]
    return jnp.concatenate([values, extra], axis=0)


def pick(terms, targets, base):
    spots = iota((CAP, targets.shape[1]), 0) + base
    return dot_nt(terms, (spots == targets).astype(F32).astype(BF16))


def fold(value, count):
    return jnp.where(value >= count, value - count, value)


def step_kernel(
    dom_count, col_count, reach, links_ref, panel_hbm, blocks_hbm, rows_ref, parts_ref,
    basis_ref, residual_ref, gram_ref,
    panel_ref, blocks_ref, load_sems, panels, terms, send, arrived, local, terms_in, landing, pieces, others, parts, sums, total,
    whole, dom_sems, col_sems, sum_sems, all_sems,
):
    dom, col = lax.axis_index("dom"), lax.axis_index("col")
    devices = dom_count * col_count
    me = dom * col_count + col
    width = panel_ref.shape[0]
    coupled_count, node, entries = blocks_ref.shape
    elements = links_ref.shape[1]
    rs = entries // elements
    group = LANES // rs
    part = ROWS_DEV // col_count
    size = width * col_count

    def remote(source, target, sems, index, device):
        return pltpu.make_async_remote_copy(
            src_ref=source,
            dst_ref=target,
            send_sem=sems.at[0, index],
            recv_sem=sems.at[1, index],
            device_id=device,
            device_id_type=pl.DeviceIdType.MESH,
        )

    def device_at(offset):
        index = fold(me + offset, devices)
        return index, (index // col_count, index % col_count)

    def dom_copy(o):
        return remote(send.at[o - 1], arrived.at[o - 1], dom_sems, o - 1, (fold(dom + o, dom_count), col))

    def col_copy(o):
        there = fold(col + o, col_count)
        return remote(pieces.at[there], others.at[col], col_sems, o - 1, (dom, there))

    def sum_copy(o):
        index, device = device_at(o)
        return remote(parts.at[index], sums.at[o - 1], sum_sems, o - 1, device)

    def all_copy(o):
        _, device = device_at(o)
        return remote(total, whole.at[me], all_sems, o - 1, device)

    panel_load = pltpu.make_async_copy(panel_hbm, panel_ref, load_sems.at[0])
    blocks_load = pltpu.make_async_copy(blocks_hbm, blocks_ref, load_sems.at[1])
    panel_load.start()
    blocks_load.start()
    barrier = pltpu.get_barrier_semaphore()

    @pl.loop(1, devices)
    def _(o):
        _, device = device_at(o)
        pl.semaphore_signal(barrier, inc=1, device_id=device, device_id_type=pl.DeviceIdType.MESH)

    shift = ROWS_DEV.bit_length() - 1
    match_rows = max(16, dom_count)
    before = (iota((LANES, LANES), 0) < iota((LANES, LANES), 1)).astype(F32).astype(BF16)
    carry = jnp.zeros((match_rows, 1), F32)
    targets = []
    for start in range(0, entries, LANES):
        rows = rows_ref[:, start : start + LANES]
        offset = fold((rows >> shift) - dom + dom_count, dom_count)
        local_row = rows & (ROWS_DEV - 1)
        matches = (iota((match_rows, LANES), 0) == offset).astype(F32)
        ranks = jnp.sum(
            matches * (dot_nn(matches.astype(BF16), before) + carry), axis=0, keepdims=True
        ).astype(jnp.int32)
        carry = carry + jnp.sum(matches, axis=1, keepdims=True)
        targets.append(
            jnp.where(offset == 0, local_row, ROWS_DEV + (offset - 1) * CAP + ranks)
        )
    targets = jnp.concatenate(targets, axis=1)

    row_values = (rows_ref[...] & (ROWS_DEV - 1)).astype(F32)
    which = iota((8, entries), 0)
    extra = jnp.where(which == 0, parts_ref[...], jnp.where(which == 1, row_values, 0.0))
    terms[2 * width :, :] = split_extra(extra)

    panel_load.wait()

    @pl.loop(0, elements // 2)
    def _(pair):
        window = panel_ref[:, pl.ds(pl.multiple_of(pair * 2 * node, LANES), 2 * node)]
        panels[2 * pair] = window[:, :node]
        panels[2 * pair + 1] = window[:, node:]

    lane_element = iota((width, LANES), 1) // rs

    blocks_load.wait()

    @pl.loop(0, elements // group)
    def _(block):
        columns = pl.ds(pl.multiple_of(block * LANES, LANES), LANES)
        found = jnp.zeros((group * width, LANES), F32)
        for coupled in range(coupled_count):
            picked = jnp.concatenate(
                [panels[links_ref[coupled, block * group + q]] for q in range(group)], axis=0
            )
            found = found + dot_nn(picked, blocks_ref[coupled, :, columns])
        out = found[:width]
        for q in range(1, group):
            out = jnp.where(lane_element == q, found[q * width : (q + 1) * width], out)
        high, low = split_values(out)
        terms[:width, columns] = high
        terms[width : 2 * width, columns] = low

    pl.semaphore_wait(barrier, devices - 1)

    @pl.loop(1, reach + 1)
    def _(o):
        send[o - 1] = join(pick(terms[...], targets, ROWS_DEV + (o - 1) * CAP), width)
        dom_copy(o).start()

    @pl.loop(0, ROWS_DEV // CAP)
    def _(tile):
        base = tile * CAP
        local[:, pl.ds(pl.multiple_of(base, CAP), CAP)] = join(
            pick(terms[...], targets, base), width
        )

    for o in range(1, reach + 1):
        dom_copy(o).wait_recv()
        columns = slice((o - 1) * CAP, o * CAP)
        high, low = split_values(arrived[o - 1, :width, :])
        terms_in[:width, columns] = high
        terms_in[width : 2 * width, columns] = low
        extra = arrived[o - 1, width:, :]
        terms_in[2 * width :, columns] = split_extra(extra)
        landing[:, columns] = extra[1:2, :].astype(jnp.int32)
    targets = landing[...]

    def assemble(base):
        columns = pl.ds(pl.multiple_of(base, CAP), CAP)
        found = join(pick(terms_in[...], targets, base), width) + local[:, columns]
        basis_ref[:, columns] = found[:width]
        residual_ref[:, columns] = found[width : width + 1]
        return found

    if part == CAP:

        @pl.loop(1, col_count)
        def _(o):
            there = fold(col + o, col_count)
            pieces[there] = assemble(there * part)[:width]
            col_copy(o).start()

        found = assemble(col * part)
        others[col] = found[:width]
        own_residual = found[width : width + 1]
    else:
        for tile in range(ROWS_DEV // CAP):
            assemble(tile * CAP)
        own_residual = jnp.zeros((1, part), F32)
        for index in range(col_count):
            columns = slice(index * part, (index + 1) * part)
            pieces[index] = basis_ref[:, columns]
            own_residual = own_residual + jnp.where(index == col, residual_ref[:, columns], 0.0)
        for o in range(1, col_count):
            col_copy(o).start()
        others[col] = pieces[col]
    for o in range(1, col_count):
        col_copy(o).wait_recv()

    basis = others[...].reshape(size, part)
    gram = dot_nt(basis, basis, HIGHEST)
    gradient = dot_nt(jnp.broadcast_to(own_residual, (8, part)), basis, HIGHEST)[:1]
    row, column = iota((size, size), 0), iota((size, size), 1)
    gram = jnp.where((row == size - 1) & (column < size - 1), gradient, gram)
    turned = pltpu.roll(jnp.broadcast_to(gradient, (8, size)), 1, axis=1)[:1]
    gram = jnp.where((row == size - 2) & (column == 0), turned, gram)
    count, height, span = parts.shape
    if span == size:
        for index in range(count):
            parts[index] = gram[index * height : (index + 1) * height]
    else:
        for index in range(count):
            start = index * span % size
            parts[index] = gram[index * span // size][None, start : start + span]

    @pl.loop(1, devices)
    def _(o):
        sum_copy(o).start()

    @pl.loop(1, devices)
    def _(o):
        sum_copy(o).wait_recv()

    mine = jnp.sum(sums[...], axis=0) + parts[me]
    total[...] = mine

    @pl.loop(1, devices)
    def _(o):
        all_copy(o).start()

    whole[me] = mine

    @pl.loop(1, devices)
    def _(o):
        all_copy(o).wait_recv()

    gram_ref[...] = whole[...]
    for o in range(1, reach + 1):
        dom_copy(o).wait_send()
    for o in range(1, col_count):
        col_copy(o).wait_send()

    @pl.loop(1, devices)
    def _(o):
        sum_copy(o).wait_send()
        all_copy(o).wait_send()


def inverse(matrix):
    size = matrix.shape[0]
    shape = (8, size)
    row, lane = iota(shape, 0), iota(shape, 1)

    def step(_, groups):
        panel = groups[0]
        columns = [jnp.broadcast_to(panel[:, j : j + 1], shape) for j in range(8)]
        work = jnp.where(lane < 8, (lane == row).astype(F32), panel)
        for i in range(8):
            here = row == i
            scale = 1.0 / jnp.broadcast_to(columns[i][i : i + 1], shape)
            factor = columns[i]
            moved = jnp.broadcast_to(work[i : i + 1], shape) * scale
            work = jnp.where(here, moved, work - factor * moved)
            for j in range(i + 1, 8):
                moved = jnp.broadcast_to(columns[j][i : i + 1], shape) * scale
                columns[j] = jnp.where(here, moved, columns[j] - factor * moved)
        spread = [jnp.broadcast_to(work[k : k + 1], shape) for k in range(8)]
        done = []
        for other in groups[1:]:
            out = jnp.where(lane < 8, 0.0, other)
            for k in range(8):
                out = out - jnp.broadcast_to(other[:, k : k + 1], shape) * spread[k]
            done.append(out)
        return tuple(pltpu.roll(x, size - 8, axis=1) for x in done + [work])

    groups = tuple(matrix[k : k + 8] for k in range(0, size, 8))
    return jnp.concatenate(lax.fori_loop(0, size // 8, step, groups, unroll=2), axis=0)


def solve_kernel(
    col_ref, gram_ref, basis_ref, residual_ref, out_ref, basis_out_ref, residual_out_ref
):
    basis_out_ref[...] = basis_ref[...]
    residual_out_ref[...] = residual_ref[...]
    size = gram_ref.shape[0]
    half = size // 2
    row, column = iota((half, half), 0), iota((half, half), 1)
    upper = row <= column

    def mirrored(block):
        block = jnp.where(upper, block, 0.0)
        return block + jnp.where(row == column, 0.0, block).T

    lane = iota((1, size), 1)
    last = jnp.sum(
        jnp.where(lane == 0, gram_ref[size - 2 : size - 1, :], 0.0), axis=1, keepdims=True
    )
    gradient = jnp.where(lane == size - 1, last, gram_ref[size - 1 : size, :])
    gradient = jnp.broadcast_to(gradient, (8, size))
    first = mirrored(gram_ref[:half, :half])
    cross = gram_ref[:half, half:]
    second = mirrored(gram_ref[half:, half:])
    first_inverse = inverse(first)
    carried = dot_nn(first_inverse, cross, HIGHEST)
    second_inverse = inverse(second - dot_tn(cross, carried, HIGHEST))

    def apply(top, bottom):
        low = dot_nt(bottom - dot_nn(top, carried, HIGHEST), second_inverse, HIGHEST)
        return dot_nt(top, first_inverse, HIGHEST) - dot_nt(low, carried, HIGHEST), low

    top, bottom = gradient[:, :half], gradient[:, half:]
    x_top, x_bottom = apply(top, bottom)
    off_top = top - dot_nn(x_top, first, HIGHEST) - dot_nt(x_bottom, cross, HIGHEST)
    off_bottom = bottom - dot_nn(x_top, cross, HIGHEST) - dot_nn(x_bottom, second, HIGHEST)
    more_top, more_bottom = apply(off_top, off_bottom)
    full = -jnp.concatenate([x_top + more_top, x_bottom + more_bottom], axis=1)[:1]
    width = out_ref.shape[1]
    out = jnp.zeros((1, width), F32)
    for index in range(size // width):
        out = jnp.where(col_ref[0] == index, full[:, index * width : (index + 1) * width], out)
    out_ref[...] = out


VMEM = pl.BlockSpec(memory_space=pltpu.VMEM)
SMEM = pl.BlockSpec(memory_space=pltpu.SMEM)
ANY = pl.BlockSpec(memory_space=pl.ANY)


def body(basis_panel, jacobian, neighbors, sample_rows, residual_parts):
    dom_count, col_count = lax.axis_size("dom"), lax.axis_size("col")
    col_index = lax.axis_index("col")
    width = basis_panel.shape[0]
    entries = sample_rows.shape[0]
    elements = neighbors.shape[0]
    node = jacobian.shape[1]
    size = width * col_count
    shape = jax.ShapeDtypeStruct
    reach = min(dom_count - 1, REACH_MOST)
    part = ROWS_DEV // col_count
    devices = dom_count * col_count
    if size % devices == 0:
        chunk = (devices, size // devices, size)
    else:
        chunk = (devices, 1, size * size // devices)
    jacobian_basis, sampled_residual, whole = pl.pallas_call(
        functools.partial(step_kernel, dom_count, col_count, reach),
        out_shape=(
            shape((width, ROWS_DEV), F32), shape((1, ROWS_DEV), F32), shape(chunk, F32)
        ),
        in_specs=[SMEM, ANY, ANY, VMEM, VMEM],
        out_specs=(VMEM, VMEM, VMEM),
        scratch_shapes=[
            pltpu.VMEM(basis_panel.shape, BF16),
            pltpu.VMEM(jacobian.shape, BF16),
            pltpu.SemaphoreType.DMA((2,)),
            pltpu.VMEM((elements, width, node), BF16),
            pltpu.VMEM((2 * width + 32, entries), BF16),
            pltpu.VMEM((reach, width + 8, CAP), F32),
            pltpu.VMEM((reach, width + 8, CAP), F32),
            pltpu.VMEM((width + 8, ROWS_DEV), F32),
            pltpu.VMEM((2 * width + 32, reach * CAP), BF16),
            pltpu.VMEM((1, reach * CAP), jnp.int32),
            pltpu.VMEM((col_count, width, part), F32),
            pltpu.VMEM((col_count, width, part), F32),
            pltpu.VMEM(chunk, F32),
            pltpu.VMEM((devices - 1,) + chunk[1:], F32),
            pltpu.VMEM(chunk[1:], F32),
            pltpu.VMEM(chunk, F32),
            pltpu.SemaphoreType.DMA((2, reach)),
            pltpu.SemaphoreType.DMA((2, col_count - 1)),
            pltpu.SemaphoreType.DMA((2, devices - 1)),
            pltpu.SemaphoreType.DMA((2, devices - 1)),
        ],
        compiler_params=pltpu.CompilerParams(collective_id=0, has_side_effects=True),
        name="step",
    )(
        neighbors.T,
        basis_panel,
        jacobian,
        sample_rows.reshape(1, entries),
        residual_parts.reshape(1, entries),
    )
    reduced_step, jacobian_basis, sampled_residual = pl.pallas_call(
        solve_kernel,
        out_shape=(
            shape((1, width), F32), shape((width, ROWS_DEV), F32), shape((1, ROWS_DEV), F32)
        ),
        in_specs=[SMEM, VMEM, VMEM, VMEM],
        out_specs=(VMEM, VMEM, VMEM),
        name="solve",
    )(
        col_index.astype(jnp.int32).reshape(1),
        whole.reshape(size, size),
        jacobian_basis,
        sampled_residual,
    )
    return (jacobian_basis, sampled_residual[0], reduced_step[0])


def solution(mesh):
    placed = (P("col", "dom"), P(None, None, "dom"), P("dom", None), P("dom"), P("dom"))
    return jax.shard_map(
        body,
        mesh=mesh,
        in_specs=placed,
        out_specs=(P("col", "dom"), P("dom"), P("col")),
        check_vma=False,
    )
```

```python
import functools

import jax
import jax.numpy as jnp
from jax import lax
from jax.experimental import pallas as pl
from jax.experimental.pallas import tpu as pltpu
from jax.sharding import PartitionSpec as P

ROWS_DEV = 1024
CAP = 256
REACH_MOST = 8
LANES = 128
HIGHEST = lax.Precision.HIGHEST
F32 = jnp.float32
BF16 = jnp.bfloat16


def iota(shape, dim):
    return lax.broadcasted_iota(jnp.int32, shape, dim)


def dot_nn(a, b, precision=None):
    return lax.dot_general(
        a, b, (((1,), (0,)), ((), ())), precision=precision, preferred_element_type=F32
    )


def dot_nt(a, b, precision=None):
    return lax.dot_general(
        a, b, (((1,), (1,)), ((), ())), precision=precision, preferred_element_type=F32
    )


def dot_tn(a, b, precision=None):
    return lax.dot_general(
        a, b, (((0,), (0,)), ((), ())), precision=precision, preferred_element_type=F32
    )


def split_values(x):
    high = x.astype(BF16)
    return high, (x - high.astype(F32)).astype(BF16)


def split_extra(x):
    high = x.astype(BF16).astype(F32)
    middle = (x - high).astype(BF16).astype(F32)
    low = x - high - middle
    return jnp.concatenate([high, middle, low, jnp.zeros_like(x)], axis=0).astype(BF16)


def join(found, width):
    values = found[:width] + found[width : 2 * width]
    base = 2 * width
    extra = found[base : base + 8] + found[base + 8 : base + 16] + found[base + 16 : base + 24]
    return jnp.concatenate([values, extra], axis=0)


def pick(terms, targets, base):
    spots = iota((CAP, targets.shape[1]), 0) + base
    return dot_nt(terms, (spots == targets).astype(F32).astype(BF16))


def fold(value, count):
    return jnp.where(value >= count, value - count, value)


def step_kernel(
    dom_count, col_count, reach, links_ref, panel_hbm, blocks_hbm, rows_ref, parts_ref,
    basis_ref, residual_ref, gram_ref,
    panel_ref, blocks_ref, load_sems, panels, terms, send, arrived, local, terms_in, landing, pieces, others, parts, paired, team_parts,
    sums, total, whole, dom_sems, col_sems, pair_sems, sum_sems, all_sems, relay_sems,
):
    dom, col = lax.axis_index("dom"), lax.axis_index("col")
    devices = dom_count * col_count
    me = dom * col_count + col
    width = panel_ref.shape[0]
    coupled_count, node, entries = blocks_ref.shape
    elements = links_ref.shape[1]
    rs = entries // elements
    group = LANES // rs
    part = ROWS_DEV // col_count
    size = width * col_count

    def remote(source, target, sems, index, device):
        return pltpu.make_async_remote_copy(
            src_ref=source,
            dst_ref=target,
            send_sem=sems.at[0, index],
            recv_sem=sems.at[1, index],
            device_id=device,
            device_id_type=pl.DeviceIdType.MESH,
        )

    def device_at(offset):
        index = fold(me + offset, devices)
        return index, (index // col_count, index % col_count)

    side, mate = dom % 2, (dom // 2 * 2 + 1 - dom % 2, col)
    team, spot = devices // 2, dom // 2 * col_count + col

    def mate_at(offset):
        index = fold(spot + offset, team)
        return index, (index // col_count * 2 + side, index % col_count)

    def dom_copy(o):
        return remote(send.at[o - 1], arrived.at[o - 1], dom_sems, o - 1, (fold(dom + o, dom_count), col))

    def col_copy(o):
        there = fold(col + o, col_count)
        return remote(pieces.at[there], others.at[col], col_sems, o - 1, (dom, there))

    def pair_copy():
        return remote(parts.at[1 - side], paired, pair_sems, 0, mate)

    def sum_copy(o):
        index, device = mate_at(o)
        return remote(team_parts.at[index], sums.at[o - 1], sum_sems, o - 1, device)

    def all_copy(o):
        _, device = mate_at(o)
        return remote(total, whole.at[side, spot], all_sems, o - 1, device)

    def relay_copy(o):
        place = whole.at[side, fold(spot - o + team, team)]
        return remote(place, place, relay_sems, o, mate)

    panel_load = pltpu.make_async_copy(panel_hbm, panel_ref, load_sems.at[0])
    blocks_load = pltpu.make_async_copy(blocks_hbm, blocks_ref, load_sems.at[1])
    panel_load.start()
    blocks_load.start()
    barrier = pltpu.get_barrier_semaphore()

    @pl.loop(1, devices)
    def _(o):
        _, device = device_at(o)
        pl.semaphore_signal(barrier, inc=1, device_id=device, device_id_type=pl.DeviceIdType.MESH)

    shift = ROWS_DEV.bit_length() - 1
    match_rows = max(16, dom_count)
    before = (iota((LANES, LANES), 0) < iota((LANES, LANES), 1)).astype(F32).astype(BF16)
    carry = jnp.zeros((match_rows, 1), F32)
    targets = []
    for start in range(0, entries, LANES):
        rows = rows_ref[:, start : start + LANES]
        offset = fold((rows >> shift) - dom + dom_count, dom_count)
        local_row = rows & (ROWS_DEV - 1)
        matches = (iota((match_rows, LANES), 0) == offset).astype(F32)
        ranks = jnp.sum(
            matches * (dot_nn(matches.astype(BF16), before) + carry), axis=0, keepdims=True
        ).astype(jnp.int32)
        carry = carry + jnp.sum(matches, axis=1, keepdims=True)
        targets.append(
            jnp.where(offset == 0, local_row, ROWS_DEV + (offset - 1) * CAP + ranks)
        )
    targets = jnp.concatenate(targets, axis=1)

    row_values = (rows_ref[...] & (ROWS_DEV - 1)).astype(F32)
    which = iota((8, entries), 0)
    extra = jnp.where(which == 0, parts_ref[...], jnp.where(which == 1, row_values, 0.0))
    terms[2 * width :, :] = split_extra(extra)

    panel_load.wait()

    @pl.loop(0, elements // 2)
    def _(pair):
        window = panel_ref[:, pl.ds(pl.multiple_of(pair * 2 * node, LANES), 2 * node)]
        panels[2 * pair] = window[:, :node]
        panels[2 * pair + 1] = window[:, node:]

    lane_element = iota((width, LANES), 1) // rs

    blocks_load.wait()

    @pl.loop(0, elements // group)
    def _(block):
        columns = pl.ds(pl.multiple_of(block * LANES, LANES), LANES)
        found = jnp.zeros((group * width, LANES), F32)
        for coupled in range(coupled_count):
            picked = jnp.concatenate(
                [panels[links_ref[coupled, block * group + q]] for q in range(group)], axis=0
            )
            found = found + dot_nn(picked, blocks_ref[coupled, :, columns])
        out = found[:width]
        for q in range(1, group):
            out = jnp.where(lane_element == q, found[q * width : (q + 1) * width], out)
        high, low = split_values(out)
        terms[:width, columns] = high
        terms[width : 2 * width, columns] = low

    pl.semaphore_wait(barrier, devices - 1)

    @pl.loop(1, reach + 1)
    def _(o):
        send[o - 1] = join(pick(terms[...], targets, ROWS_DEV + (o - 1) * CAP), width)
        dom_copy(o).start()

    @pl.loop(0, ROWS_DEV // CAP)
    def _(tile):
        base = tile * CAP
        local[:, pl.ds(pl.multiple_of(base, CAP), CAP)] = join(
            pick(terms[...], targets, base), width
        )

    for o in range(1, reach + 1):
        dom_copy(o).wait_recv()
        columns = slice((o - 1) * CAP, o * CAP)
        high, low = split_values(arrived[o - 1, :width, :])
        terms_in[:width, columns] = high
        terms_in[width : 2 * width, columns] = low
        extra = arrived[o - 1, width:, :]
        terms_in[2 * width :, columns] = split_extra(extra)
        landing[:, columns] = extra[1:2, :].astype(jnp.int32)
    targets = landing[...]

    def assemble(base):
        columns = pl.ds(pl.multiple_of(base, CAP), CAP)
        found = join(pick(terms_in[...], targets, base), width) + local[:, columns]
        basis_ref[:, columns] = found[:width]
        residual_ref[:, columns] = found[width : width + 1]
        return found

    if part == CAP:

        @pl.loop(1, col_count)
        def _(o):
            there = fold(col + o, col_count)
            pieces[there] = assemble(there * part)[:width]
            col_copy(o).start()

        found = assemble(col * part)
        others[col] = found[:width]
        own_residual = found[width : width + 1]
    else:
        for tile in range(ROWS_DEV // CAP):
            assemble(tile * CAP)
        own_residual = jnp.zeros((1, part), F32)
        for index in range(col_count):
            columns = slice(index * part, (index + 1) * part)
            pieces[index] = basis_ref[:, columns]
            own_residual = own_residual + jnp.where(index == col, residual_ref[:, columns], 0.0)
        for o in range(1, col_count):
            col_copy(o).start()
        others[col] = pieces[col]
    for o in range(1, col_count):
        col_copy(o).wait_recv()

    basis = others[...].reshape(size, part)
    gram = dot_nt(basis, basis, HIGHEST)
    gradient = dot_nt(jnp.broadcast_to(own_residual, (8, part)), basis, HIGHEST)[:1]
    row, column = iota((size, size), 0), iota((size, size), 1)
    gram = jnp.where((row == size - 1) & (column < size - 1), gradient, gram)
    turned = pltpu.roll(jnp.broadcast_to(gradient, (8, size)), 1, axis=1)[:1]
    gram = jnp.where((row == size - 2) & (column == 0), turned, gram)
    _, count, height, span = parts.shape
    for half in range(2):
        for index in range(count):
            if span == size:
                start = (half * count + index) * height
                parts[half, index] = gram[start : start + height]
            else:
                start = (half * count + index) * span
                lane = start % size
                parts[half, index] = gram[start // size][None, lane : lane + span]
    pair_copy().start()
    pair_copy().wait_recv()
    team_parts[...] = parts[side] + paired[...]

    @pl.loop(1, team)
    def _(o):
        sum_copy(o).start()

    @pl.loop(1, team)
    def _(o):
        sum_copy(o).wait_recv()

    mine = jnp.sum(sums[...], axis=0) + team_parts[spot]
    total[...] = mine

    @pl.loop(1, team)
    def _(o):
        all_copy(o).start()

    whole[side, spot] = mine
    relay_copy(0).start()

    @pl.loop(1, team)
    def _(o):
        all_copy(o).wait_recv()
        relay_copy(o).start()

    @pl.loop(0, team)
    def _(o):
        back = whole.at[1 - side, fold(spot - o + team, team)]
        remote(back, back, relay_sems, o, mate).wait_recv()

    gram_ref[...] = whole[...]
    for o in range(1, reach + 1):
        dom_copy(o).wait_send()
    for o in range(1, col_count):
        col_copy(o).wait_send()

    pair_copy().wait_send()

    @pl.loop(1, team)
    def _(o):
        sum_copy(o).wait_send()
        all_copy(o).wait_send()

    @pl.loop(0, team)
    def _(o):
        relay_copy(o).wait_send()


def inverse(matrix):
    size = matrix.shape[0]
    shape = (8, size)
    row, lane = iota(shape, 0), iota(shape, 1)

    def step(_, groups):
        panel = groups[0]
        columns = [jnp.broadcast_to(panel[:, j : j + 1], shape) for j in range(8)]
        work = jnp.where(lane < 8, (lane == row).astype(F32), panel)
        for i in range(8):
            here = row == i
            scale = 1.0 / jnp.broadcast_to(columns[i][i : i + 1], shape)
            factor = columns[i]
            moved = jnp.broadcast_to(work[i : i + 1], shape) * scale
            work = jnp.where(here, moved, work - factor * moved)
            for j in range(i + 1, 8):
                moved = jnp.broadcast_to(columns[j][i : i + 1], shape) * scale
                columns[j] = jnp.where(here, moved, columns[j] - factor * moved)
        spread = [jnp.broadcast_to(work[k : k + 1], shape) for k in range(8)]
        done = []
        for other in groups[1:]:
            out = jnp.where(lane < 8, 0.0, other)
            for k in range(8):
                out = out - jnp.broadcast_to(other[:, k : k + 1], shape) * spread[k]
            done.append(out)
        return tuple(pltpu.roll(x, size - 8, axis=1) for x in done + [work])

    groups = tuple(matrix[k : k + 8] for k in range(0, size, 8))
    return jnp.concatenate(lax.fori_loop(0, size // 8, step, groups, unroll=2), axis=0)


def solve_kernel(
    col_ref, gram_ref, basis_ref, residual_ref, out_ref, basis_out_ref, residual_out_ref
):
    basis_out_ref[...] = basis_ref[...]
    residual_out_ref[...] = residual_ref[...]
    size = gram_ref.shape[0]
    half = size // 2
    row, column = iota((half, half), 0), iota((half, half), 1)
    upper = row <= column

    def mirrored(block):
        block = jnp.where(upper, block, 0.0)
        return block + jnp.where(row == column, 0.0, block).T

    lane = iota((1, size), 1)
    last = jnp.sum(
        jnp.where(lane == 0, gram_ref[size - 2 : size - 1, :], 0.0), axis=1, keepdims=True
    )
    gradient = jnp.where(lane == size - 1, last, gram_ref[size - 1 : size, :])
    gradient = jnp.broadcast_to(gradient, (8, size))
    first = mirrored(gram_ref[:half, :half])
    cross = gram_ref[:half, half:]
    second = mirrored(gram_ref[half:, half:])
    first_inverse = inverse(first)
    carried = dot_nn(first_inverse, cross, HIGHEST)
    second_inverse = inverse(second - dot_tn(cross, carried, HIGHEST))

    def apply(top, bottom):
        low = dot_nt(bottom - dot_nn(top, carried, HIGHEST), second_inverse, HIGHEST)
        return dot_nt(top, first_inverse, HIGHEST) - dot_nt(low, carried, HIGHEST), low

    top, bottom = gradient[:, :half], gradient[:, half:]
    x_top, x_bottom = apply(top, bottom)
    full = -jnp.concatenate([x_top, x_bottom], axis=1)[:1]
    width = out_ref.shape[1]
    out = jnp.zeros((1, width), F32)
    for index in range(size // width):
        out = jnp.where(col_ref[0] == index, full[:, index * width : (index + 1) * width], out)
    out_ref[...] = out


VMEM = pl.BlockSpec(memory_space=pltpu.VMEM)
SMEM = pl.BlockSpec(memory_space=pltpu.SMEM)
ANY = pl.BlockSpec(memory_space=pl.ANY)


def body(basis_panel, jacobian, neighbors, sample_rows, residual_parts):
    dom_count, col_count = lax.axis_size("dom"), lax.axis_size("col")
    col_index = lax.axis_index("col")
    width = basis_panel.shape[0]
    entries = sample_rows.shape[0]
    elements = neighbors.shape[0]
    node = jacobian.shape[1]
    size = width * col_count
    shape = jax.ShapeDtypeStruct
    reach = min(dom_count - 1, REACH_MOST)
    part = ROWS_DEV // col_count
    devices = dom_count * col_count
    team = devices // 2
    if size % devices == 0:
        chunk = (2, team, size // devices, size)
    else:
        chunk = (2, team, 1, size * size // devices)
    jacobian_basis, sampled_residual, whole = pl.pallas_call(
        functools.partial(step_kernel, dom_count, col_count, reach),
        out_shape=(
            shape((width, ROWS_DEV), F32), shape((1, ROWS_DEV), F32), shape(chunk, F32)
        ),
        in_specs=[SMEM, ANY, ANY, VMEM, VMEM],
        out_specs=(VMEM, VMEM, VMEM),
        scratch_shapes=[
            pltpu.VMEM(basis_panel.shape, BF16),
            pltpu.VMEM(jacobian.shape, BF16),
            pltpu.SemaphoreType.DMA((2,)),
            pltpu.VMEM((elements, width, node), BF16),
            pltpu.VMEM((2 * width + 32, entries), BF16),
            pltpu.VMEM((reach, width + 8, CAP), F32),
            pltpu.VMEM((reach, width + 8, CAP), F32),
            pltpu.VMEM((width + 8, ROWS_DEV), F32),
            pltpu.VMEM((2 * width + 32, reach * CAP), BF16),
            pltpu.VMEM((1, reach * CAP), jnp.int32),
            pltpu.VMEM((col_count, width, part), F32),
            pltpu.VMEM((col_count, width, part), F32),
            pltpu.VMEM(chunk, F32),
            pltpu.VMEM(chunk[1:], F32),
            pltpu.VMEM(chunk[1:], F32),
            pltpu.VMEM((team - 1,) + chunk[2:], F32),
            pltpu.VMEM(chunk[2:], F32),
            pltpu.VMEM(chunk, F32),
            pltpu.SemaphoreType.DMA((2, reach)),
            pltpu.SemaphoreType.DMA((2, col_count - 1)),
            pltpu.SemaphoreType.DMA((2, 1)),
            pltpu.SemaphoreType.DMA((2, team - 1)),
            pltpu.SemaphoreType.DMA((2, team - 1)),
            pltpu.SemaphoreType.DMA((2, team)),
        ],
        compiler_params=pltpu.CompilerParams(collective_id=0, has_side_effects=True),
        name="step",
    )(
        neighbors.T,
        basis_panel,
        jacobian,
        sample_rows.reshape(1, entries),
        residual_parts.reshape(1, entries),
    )
    reduced_step, jacobian_basis, sampled_residual = pl.pallas_call(
        solve_kernel,
        out_shape=(
            shape((1, width), F32), shape((width, ROWS_DEV), F32), shape((1, ROWS_DEV), F32)
        ),
        in_specs=[SMEM, VMEM, VMEM, VMEM],
        out_specs=(VMEM, VMEM, VMEM),
        name="solve",
    )(
        col_index.astype(jnp.int32).reshape(1),
        whole.reshape(size, size),
        jacobian_basis,
        sampled_residual,
    )
    return (jacobian_basis, sampled_residual[0], reduced_step[0])


def solution(mesh):
    placed = (P("col", "dom"), P(None, None, "dom"), P("dom", None), P("dom"), P("dom"))
    return jax.shard_map(
        body,
        mesh=mesh,
        in_specs=placed,
        out_specs=(P("col", "dom"), P("dom"), P("col")),
        check_vma=False,
    )
```

```python
import functools

import jax
import jax.numpy as jnp
from jax import lax
from jax.experimental import pallas as pl
from jax.experimental.pallas import tpu as pltpu
from jax.sharding import PartitionSpec as P

ROWS_DEV = 1024
CAP = 256
REACH_MOST = 8
LANES = 128
HIGHEST = lax.Precision.HIGHEST
F32 = jnp.float32
BF16 = jnp.bfloat16


def iota(shape, dim):
    return lax.broadcasted_iota(jnp.int32, shape, dim)


def dot_nn(a, b, precision=None):
    return lax.dot_general(
        a, b, (((1,), (0,)), ((), ())), precision=precision, preferred_element_type=F32
    )


def dot_nt(a, b, precision=None):
    return lax.dot_general(
        a, b, (((1,), (1,)), ((), ())), precision=precision, preferred_element_type=F32
    )


def dot_tn(a, b, precision=None):
    return lax.dot_general(
        a, b, (((0,), (0,)), ((), ())), precision=precision, preferred_element_type=F32
    )


def split_values(x):
    high = x.astype(BF16)
    return high, (x - high.astype(F32)).astype(BF16)


def split_extra(x):
    high = x.astype(BF16).astype(F32)
    middle = (x - high).astype(BF16).astype(F32)
    low = x - high - middle
    return jnp.concatenate([high, middle, low, jnp.zeros_like(x)], axis=0).astype(BF16)


def join(found, width):
    values = found[:width] + found[width : 2 * width]
    base = 2 * width
    extra = found[base : base + 8] + found[base + 8 : base + 16] + found[base + 16 : base + 24]
    return jnp.concatenate([values, extra], axis=0)


def pick(terms, targets, base):
    spots = iota((CAP, targets.shape[1]), 0) + base
    return dot_nt(terms, (spots == targets).astype(F32).astype(BF16))


def fold(value, count):
    return jnp.where(value >= count, value - count, value)


def step_kernel(
    dom_count, col_count, reach, links_ref, panel_hbm, blocks_hbm, rows_ref, parts_ref,
    basis_ref, residual_ref, gram_ref,
    panel_ref, blocks_ref, load_sems, panels, terms, send, arrived, local, terms_in, landing, pieces, others, parts, paired, team_parts,
    sums, total, whole, dom_sems, col_sems, pair_sems, sum_sems, all_sems, relay_sems,
):
    dom, col = lax.axis_index("dom"), lax.axis_index("col")
    devices = dom_count * col_count
    me = dom * col_count + col
    width = panel_ref.shape[0]
    coupled_count, node, entries = blocks_ref.shape
    elements = links_ref.shape[1]
    rs = entries // elements
    group = LANES // rs
    part = ROWS_DEV // col_count
    size = width * col_count

    def remote(source, target, sems, index, device):
        return pltpu.make_async_remote_copy(
            src_ref=source,
            dst_ref=target,
            send_sem=sems.at[0, index],
            recv_sem=sems.at[1, index],
            device_id=device,
            device_id_type=pl.DeviceIdType.MESH,
        )

    def device_at(offset):
        index = fold(me + offset, devices)
        return index, (index // col_count, index % col_count)

    side, mate = dom % 2, (dom // 2 * 2 + 1 - dom % 2, col)
    team, spot = devices // 2, dom // 2 * col_count + col

    def mate_at(offset):
        index = fold(spot + offset, team)
        return index, (index // col_count * 2 + side, index % col_count)

    def dom_copy(o):
        return remote(send.at[o - 1], arrived.at[o - 1], dom_sems, o - 1, (fold(dom + o, dom_count), col))

    def col_copy(o):
        there = fold(col + o, col_count)
        return remote(pieces.at[there], others.at[col], col_sems, o - 1, (dom, there))

    def pair_copy():
        return remote(parts.at[1 - side], paired, pair_sems, 0, mate)

    def sum_copy(o):
        index, device = mate_at(o)
        return remote(team_parts.at[index], sums.at[o - 1], sum_sems, o - 1, device)

    def all_copy(o):
        _, device = mate_at(o)
        return remote(total, whole.at[side, spot], all_sems, o - 1, device)

    def relay_copy(o):
        place = whole.at[side, fold(spot - o + team, team)]
        return remote(place, place, relay_sems, o, mate)

    panel_load = pltpu.make_async_copy(panel_hbm, panel_ref, load_sems.at[0])
    blocks_load = pltpu.make_async_copy(blocks_hbm, blocks_ref, load_sems.at[1])
    panel_load.start()
    blocks_load.start()
    barrier = pltpu.get_barrier_semaphore()

    @pl.loop(1, devices)
    def _(o):
        _, device = device_at(o)
        pl.semaphore_signal(barrier, inc=1, device_id=device, device_id_type=pl.DeviceIdType.MESH)

    shift = ROWS_DEV.bit_length() - 1
    match_rows = max(16, dom_count)
    before = (iota((LANES, LANES), 0) < iota((LANES, LANES), 1)).astype(F32).astype(BF16)
    carry = jnp.zeros((match_rows, 1), F32)
    targets = []
    for start in range(0, entries, LANES):
        rows = rows_ref[:, start : start + LANES]
        offset = fold((rows >> shift) - dom + dom_count, dom_count)
        local_row = rows & (ROWS_DEV - 1)
        matches = (iota((match_rows, LANES), 0) == offset).astype(F32)
        ranks = jnp.sum(
            matches * (dot_nn(matches.astype(BF16), before) + carry), axis=0, keepdims=True
        ).astype(jnp.int32)
        carry = carry + jnp.sum(matches, axis=1, keepdims=True)
        targets.append(
            jnp.where(offset == 0, local_row, ROWS_DEV + (offset - 1) * CAP + ranks)
        )
    targets = jnp.concatenate(targets, axis=1)

    row_values = (rows_ref[...] & (ROWS_DEV - 1)).astype(F32)
    which = iota((8, entries), 0)
    extra = jnp.where(which == 0, parts_ref[...], jnp.where(which == 1, row_values, 0.0))
    terms[2 * width :, :] = split_extra(extra)

    panel_load.wait()

    @pl.loop(0, elements // 2, unroll=4)
    def _(pair):
        window = panel_ref[:, pl.ds(pl.multiple_of(pair * 2 * node, LANES), 2 * node)]
        panels[2 * pair] = window[:, :node]
        panels[2 * pair + 1] = window[:, node:]

    lane_element = iota((width, LANES), 1) // rs

    blocks_load.wait()

    @pl.loop(0, elements // group, unroll=4)
    def _(block):
        columns = pl.ds(pl.multiple_of(block * LANES, LANES), LANES)
        found = jnp.zeros((group * width, LANES), F32)
        for coupled in range(coupled_count):
            picked = jnp.concatenate(
                [panels[links_ref[coupled, block * group + q]] for q in range(group)], axis=0
            )
            found = found + dot_nn(picked, blocks_ref[coupled, :, columns])
        out = found[:width]
        for q in range(1, group):
            out = jnp.where(lane_element == q, found[q * width : (q + 1) * width], out)
        high, low = split_values(out)
        terms[:width, columns] = high
        terms[width : 2 * width, columns] = low

    pl.semaphore_wait(barrier, devices - 1)

    @pl.loop(1, reach + 1)
    def _(o):
        send[o - 1] = join(pick(terms[...], targets, ROWS_DEV + (o - 1) * CAP), width)
        dom_copy(o).start()

    @pl.loop(0, ROWS_DEV // CAP)
    def _(tile):
        base = tile * CAP
        local[:, pl.ds(pl.multiple_of(base, CAP), CAP)] = join(
            pick(terms[...], targets, base), width
        )

    for o in range(1, reach + 1):
        dom_copy(o).wait_recv()
        columns = slice((o - 1) * CAP, o * CAP)
        high, low = split_values(arrived[o - 1, :width, :])
        terms_in[:width, columns] = high
        terms_in[width : 2 * width, columns] = low
        extra = arrived[o - 1, width:, :]
        terms_in[2 * width :, columns] = split_extra(extra)
        landing[:, columns] = extra[1:2, :].astype(jnp.int32)
    targets = landing[...]

    def assemble(base):
        columns = pl.ds(pl.multiple_of(base, CAP), CAP)
        found = join(pick(terms_in[...], targets, base), width) + local[:, columns]
        basis_ref[:, columns] = found[:width]
        residual_ref[:, columns] = found[width : width + 1]
        return found

    if part == CAP:

        @pl.loop(1, col_count)
        def _(o):
            there = fold(col + o, col_count)
            pieces[there] = assemble(there * part)[:width]
            col_copy(o).start()

        found = assemble(col * part)
        others[col] = found[:width]
        own_residual = found[width : width + 1]
    else:
        for tile in range(ROWS_DEV // CAP):
            assemble(tile * CAP)
        own_residual = jnp.zeros((1, part), F32)
        for index in range(col_count):
            columns = slice(index * part, (index + 1) * part)
            pieces[index] = basis_ref[:, columns]
            own_residual = own_residual + jnp.where(index == col, residual_ref[:, columns], 0.0)
        for o in range(1, col_count):
            col_copy(o).start()
        others[col] = pieces[col]
    for o in range(1, col_count):
        col_copy(o).wait_recv()

    basis = others[...].reshape(size, part)
    gram = dot_nt(basis, basis, HIGHEST)
    gradient = dot_nt(jnp.broadcast_to(own_residual, (8, part)), basis, HIGHEST)[:1]
    row, column = iota((size, size), 0), iota((size, size), 1)
    gram = jnp.where((row == size - 1) & (column < size - 1), gradient, gram)
    turned = pltpu.roll(jnp.broadcast_to(gradient, (8, size)), 1, axis=1)[:1]
    gram = jnp.where((row == size - 2) & (column == 0), turned, gram)
    _, count, height, span = parts.shape
    for half in range(2):
        for index in range(count):
            if span == size:
                start = (half * count + index) * height
                parts[half, index] = gram[start : start + height]
            else:
                start = (half * count + index) * span
                lane = start % size
                parts[half, index] = gram[start // size][None, lane : lane + span]
    pair_copy().start()
    pair_copy().wait_recv()
    team_parts[...] = parts[side] + paired[...]

    @pl.loop(1, team)
    def _(o):
        sum_copy(o).start()

    @pl.loop(1, team)
    def _(o):
        sum_copy(o).wait_recv()

    mine = jnp.sum(sums[...], axis=0) + team_parts[spot]
    total[...] = mine

    @pl.loop(1, team)
    def _(o):
        all_copy(o).start()

    whole[side, spot] = mine
    relay_copy(0).start()

    @pl.loop(1, team)
    def _(o):
        all_copy(o).wait_recv()
        relay_copy(o).start()

    @pl.loop(0, team)
    def _(o):
        back = whole.at[1 - side, fold(spot - o + team, team)]
        remote(back, back, relay_sems, o, mate).wait_recv()

    gram_ref[...] = whole[...]
    for o in range(1, reach + 1):
        dom_copy(o).wait_send()
    for o in range(1, col_count):
        col_copy(o).wait_send()

    pair_copy().wait_send()

    @pl.loop(1, team)
    def _(o):
        sum_copy(o).wait_send()
        all_copy(o).wait_send()

    @pl.loop(0, team)
    def _(o):
        relay_copy(o).wait_send()


def inverse(matrix):
    size = matrix.shape[0]
    shape = (8, size)
    row, lane = iota(shape, 0), iota(shape, 1)

    def step(_, groups):
        panel = groups[0]
        columns = [jnp.broadcast_to(panel[:, j : j + 1], shape) for j in range(8)]
        work = jnp.where(lane < 8, (lane == row).astype(F32), panel)
        for i in range(8):
            here = row == i
            scale = 1.0 / jnp.broadcast_to(columns[i][i : i + 1], shape)
            factor = columns[i]
            moved = jnp.broadcast_to(work[i : i + 1], shape) * scale
            work = jnp.where(here, moved, work - factor * moved)
            for j in range(i + 1, 8):
                moved = jnp.broadcast_to(columns[j][i : i + 1], shape) * scale
                columns[j] = jnp.where(here, moved, columns[j] - factor * moved)
        spread = [jnp.broadcast_to(work[k : k + 1], shape) for k in range(8)]
        done = []
        for other in groups[1:]:
            out = jnp.where(lane < 8, 0.0, other)
            for k in range(8):
                out = out - jnp.broadcast_to(other[:, k : k + 1], shape) * spread[k]
            done.append(out)
        return tuple(pltpu.roll(x, size - 8, axis=1) for x in done + [work])

    groups = tuple(matrix[k : k + 8] for k in range(0, size, 8))
    return jnp.concatenate(lax.fori_loop(0, size // 8, step, groups, unroll=4), axis=0)


def solve_kernel(
    col_ref, gram_ref, basis_ref, residual_ref, out_ref, basis_out_ref, residual_out_ref
):
    basis_out_ref[...] = basis_ref[...]
    residual_out_ref[...] = residual_ref[...]
    size = gram_ref.shape[0]
    half = size // 2
    row, column = iota((half, half), 0), iota((half, half), 1)
    upper = row <= column

    def mirrored(block):
        block = jnp.where(upper, block, 0.0)
        return block + jnp.where(row == column, 0.0, block).T

    lane = iota((1, size), 1)
    last = jnp.sum(
        jnp.where(lane == 0, gram_ref[size - 2 : size - 1, :], 0.0), axis=1, keepdims=True
    )
    gradient = jnp.where(lane == size - 1, last, gram_ref[size - 1 : size, :])
    gradient = jnp.broadcast_to(gradient, (8, size))
    first = mirrored(gram_ref[:half, :half])
    cross = gram_ref[:half, half:]
    second = mirrored(gram_ref[half:, half:])
    first_inverse = inverse(first)
    carried = dot_nn(first_inverse, cross, HIGHEST)
    second_inverse = inverse(second - dot_tn(cross, carried, HIGHEST))

    def apply(top, bottom):
        low = dot_nt(bottom - dot_nn(top, carried, HIGHEST), second_inverse, HIGHEST)
        return dot_nt(top, first_inverse, HIGHEST) - dot_nt(low, carried, HIGHEST), low

    top, bottom = gradient[:, :half], gradient[:, half:]
    x_top, x_bottom = apply(top, bottom)
    full = -jnp.concatenate([x_top, x_bottom], axis=1)[:1]
    width = out_ref.shape[1]
    out = jnp.zeros((1, width), F32)
    for index in range(size // width):
        out = jnp.where(col_ref[0] == index, full[:, index * width : (index + 1) * width], out)
    out_ref[...] = out


VMEM = pl.BlockSpec(memory_space=pltpu.VMEM)
SMEM = pl.BlockSpec(memory_space=pltpu.SMEM)
ANY = pl.BlockSpec(memory_space=pl.ANY)


def body(basis_panel, jacobian, neighbors, sample_rows, residual_parts):
    dom_count, col_count = lax.axis_size("dom"), lax.axis_size("col")
    col_index = lax.axis_index("col")
    width = basis_panel.shape[0]
    entries = sample_rows.shape[0]
    elements = neighbors.shape[0]
    node = jacobian.shape[1]
    size = width * col_count
    shape = jax.ShapeDtypeStruct
    reach = min(dom_count - 1, REACH_MOST)
    part = ROWS_DEV // col_count
    devices = dom_count * col_count
    team = devices // 2
    if size % devices == 0:
        chunk = (2, team, size // devices, size)
    else:
        chunk = (2, team, 1, size * size // devices)
    jacobian_basis, sampled_residual, whole = pl.pallas_call(
        functools.partial(step_kernel, dom_count, col_count, reach),
        out_shape=(
            shape((width, ROWS_DEV), F32), shape((1, ROWS_DEV), F32), shape(chunk, F32)
        ),
        in_specs=[SMEM, ANY, ANY, VMEM, VMEM],
        out_specs=(VMEM, VMEM, VMEM),
        scratch_shapes=[
            pltpu.VMEM(basis_panel.shape, BF16),
            pltpu.VMEM(jacobian.shape, BF16),
            pltpu.SemaphoreType.DMA((2,)),
            pltpu.VMEM((elements, width, node), BF16),
            pltpu.VMEM((2 * width + 32, entries), BF16),
            pltpu.VMEM((reach, width + 8, CAP), F32),
            pltpu.VMEM((reach, width + 8, CAP), F32),
            pltpu.VMEM((width + 8, ROWS_DEV), F32),
            pltpu.VMEM((2 * width + 32, reach * CAP), BF16),
            pltpu.VMEM((1, reach * CAP), jnp.int32),
            pltpu.VMEM((col_count, width, part), F32),
            pltpu.VMEM((col_count, width, part), F32),
            pltpu.VMEM(chunk, F32),
            pltpu.VMEM(chunk[1:], F32),
            pltpu.VMEM(chunk[1:], F32),
            pltpu.VMEM((team - 1,) + chunk[2:], F32),
            pltpu.VMEM(chunk[2:], F32),
            pltpu.VMEM(chunk, F32),
            pltpu.SemaphoreType.DMA((2, reach)),
            pltpu.SemaphoreType.DMA((2, col_count - 1)),
            pltpu.SemaphoreType.DMA((2, 1)),
            pltpu.SemaphoreType.DMA((2, team - 1)),
            pltpu.SemaphoreType.DMA((2, team - 1)),
            pltpu.SemaphoreType.DMA((2, team)),
        ],
        compiler_params=pltpu.CompilerParams(collective_id=0, has_side_effects=True),
        name="step",
    )(
        neighbors.T,
        basis_panel,
        jacobian,
        sample_rows.reshape(1, entries),
        residual_parts.reshape(1, entries),
    )
    reduced_step, jacobian_basis, sampled_residual = pl.pallas_call(
        solve_kernel,
        out_shape=(
            shape((1, width), F32), shape((width, ROWS_DEV), F32), shape((1, ROWS_DEV), F32)
        ),
        in_specs=[SMEM, VMEM, VMEM, VMEM],
        out_specs=(VMEM, VMEM, VMEM),
        name="solve",
    )(
        col_index.astype(jnp.int32).reshape(1),
        whole.reshape(size, size),
        jacobian_basis,
        sampled_residual,
    )
    return (jacobian_basis, sampled_residual[0], reduced_step[0])


def solution(mesh):
    placed = (P("col", "dom"), P(None, None, "dom"), P("dom", None), P("dom"), P("dom"))
    return jax.shard_map(
        body,
        mesh=mesh,
        in_specs=placed,
        out_specs=(P("col", "dom"), P("dom"), P("col")),
        check_vma=False,
    )
```
